32 devices in a mesh: groups: 2 (over y), dp: 4 (over z), tensor: 2 (over x), layer: 2 (over core).
Axes of the slice: x: 2, y: 2, z: 4, core: 2. Of those that a mesh axis runs over, the one named last changes fastest.
Arguments:
- train_inputs: bfloat16 [2, 256, 16, 8192], P('layer', ('groups', 'dp'), None, 'tensor'), parts along dimension 1, may hold values from -6 to 6
- train_grads: bfloat16 [2, 256, 16, 8192], P('layer', ('groups', 'dp'), None, 'tensor'), parts along dimension 1, may hold values from -6 to 6
- bench_inputs: bfloat16 [2, 128, 16, 8192], P('layer', ('groups', 'dp'), None, 'tensor'), parts along dimension 1, may hold values from -6 to 6
- bench_grads: bfloat16 [2, 128, 16, 8192], P('layer', ('groups', 'dp'), None, 'tensor'), parts along dimension 1, may hold values from -6 to 6
- answer_mask: int32 [128, 16], P(('groups', 'dp')), parts along dimension 0, may hold values 0 or 1
- factors: bfloat16 [2, 8192, 128], P('layer', 'tensor'), may hold values from -0.0625 to 0.0625
- precond: bfloat16 [2, 4096, 4096], P('layer', None, ('dp', 'tensor')), may hold values from -0.09375 to 0.09375
Outputs:
- scores: float32 [256, 64], P(('groups', 'dp', 'tensor', 'layer')), parts along dimension 0
The draws below stay inside these ranges and needn't reach their ends.
There are 2 independent parts, one for each index of `groups`. The reference program is written for one: setup_inputs(seed, part) draws one part's arguments, and reference() takes and returns one part's arrays. A program takes and returns all parts, laid end to end along the dimension named above; an argument that names none is the same for every part. Nothing has to cross between parts.
All inputs are finite; a program needn't handle non-finite values. No bound on the sum of `answer_mask` on one device may be relied on, other than what follows from the above.
Results may differ from the reference program's by a relative error of at most 0.005.
Values may be sent and summed in bfloat16 or wider, within the bound.
A program may use at most 64 MiB of HBM per device.

```python
import math
import jax
import jax.numpy as jnp
from jax import lax

D = 8192
K = 64
SEQ = 16
F = 4096
TRAIN = 128
BENCH = 64
LAYERS = 2


def set_ends(entries, rng, smallest, high):
    shape = entries.shape
    index_at = [jax.random.randint(jax.random.fold_in(rng, axis), (), 0, shape[axis]) for axis in range(len(shape))]
    entries = entries.at[tuple(index_at)].set(smallest)
    longest = shape.index(max(shape))
    index_at[longest] = (index_at[longest] + 1) % shape[longest]
    return entries.at[tuple(index_at)].set(high)


def levels(rng, extent, cuts, smallest, largest):
    def one(position, parts):
        draws = jax.random.uniform(jax.random.fold_in(jax.random.fold_in(rng, 6), position), (parts,), jnp.float32, smallest / len(cuts), largest / len(cuts))
        return jnp.repeat(jnp.exp(draws), extent[position] // parts).reshape((-1,) + (1,) * (len(extent) - position - 1))

    loudness = one(*cuts[0])
    for cut in cuts[1:]:
        loudness = loudness * one(*cut)
    return loudness


def normal_values(stream_key, dims, deviation, bound, cuts=(), kind=jnp.bfloat16):
    level = levels(stream_key, dims, cuts, -0.22, 0.18) if cuts else 1.0
    values = jax.random.normal(stream_key, dims, jnp.float32) * deviation * level
    return jnp.minimum(jnp.maximum(values, -bound), bound).astype(kind)


def setup_inputs(seed: int = 0, part: int = 0) -> dict:
    key_list = jax.random.split(jax.random.key(seed), 8)
    part_keys = jax.random.split(jax.random.fold_in(key_list[7], part), 8)
    return {
        "train_inputs": normal_values(part_keys[0], (LAYERS, TRAIN, SEQ, D), 1.0, 6.0, ((0, 2), (1, 4), (3, 2))),
        "train_grads": normal_values(part_keys[1], (LAYERS, TRAIN, SEQ, D), 1.0, 6.0, ((0, 2), (1, 4), (3, 2))),
        "bench_inputs": normal_values(part_keys[2], (LAYERS, BENCH, SEQ, D), 1.0, 6.0, ((0, 2), (1, 4), (3, 2))),
        "bench_grads": normal_values(part_keys[3], (LAYERS, BENCH, SEQ, D), 1.0, 6.0, ((0, 2), (1, 4), (3, 2))),
        "answer_mask": set_ends((jax.random.randint(part_keys[4], (BENCH, SEQ), 0, 2) < 1).astype(jnp.int32), jax.random.fold_in(part_keys[4], 1), 0, 1),
        "factors": normal_values(key_list[5], (LAYERS, D, 2 * K), D ** -0.5, 0.0625, ((0, 2), (1, 2))),
        "precond": normal_values(key_list[6], (LAYERS, F, F), F ** -0.5, 0.09375, ((0, 2), (2, 8))),
    }


def features(inputs_here, grads_here, factor):
    examples = inputs_here.shape[0]
    in_proj = jnp.dot(inputs_here.reshape(examples * SEQ, D), factor[:, :K], preferred_element_type=jnp.float32)
    out_proj = jnp.dot(grads_here.reshape(examples * SEQ, D), factor[:, K:], preferred_element_type=jnp.float32)
    in_proj = in_proj.reshape(examples, SEQ, K)
    out_proj = out_proj.reshape(examples, SEQ, K)
    outer = jnp.einsum('esa,esb->eab', out_proj, in_proj, precision=lax.Precision.HIGHEST) / math.sqrt(SEQ)
    return outer.reshape(examples, K * K).astype(jnp.bfloat16)

def reference(train_inputs, train_grads, bench_inputs, bench_grads, answer_mask, factors, precond):
    total = jnp.zeros((TRAIN, BENCH), jnp.float32)
    mask_values = answer_mask.astype(jnp.bfloat16)[:, :, None]
    for level in range(LAYERS):
        train_feats = features(train_inputs[level], train_grads[level], factors[level])
        bench_feats = features(bench_inputs[level], bench_grads[level] * mask_values, factors[level])
        bench_pre = jnp.dot(bench_feats, precond[level], preferred_element_type=jnp.float32).astype(jnp.bfloat16)
        total = total + jnp.dot(train_feats, bench_pre.T, preferred_element_type=jnp.float32)
    return total / math.sqrt(K * K * LAYERS)
```

```python
import functools
import math

import jax
import jax.numpy as jnp
from jax import lax
from jax.experimental import pallas as pl
from jax.experimental.pallas import tpu as pltpu
from jax.sharding import PartitionSpec as P

MESH = pl.DeviceIdType.MESH


def project(inputs_here, grads_here, factor):
    examples, length, shard_width = inputs_here.shape
    factor_width = factor.shape[1] // 2
    in_proj = jnp.dot(
        inputs_here.reshape(examples * length, shard_width),
        factor[:, :factor_width],
        preferred_element_type=jnp.float32,
    )
    out_proj = jnp.dot(
        grads_here.reshape(examples * length, shard_width),
        factor[:, factor_width:],
        preferred_element_type=jnp.float32,
    )
    return jnp.concatenate([in_proj, out_proj], axis=1)


def outer_features(token_rows, examples, length, factor_width):
    grouped = token_rows.reshape(examples, length, 2 * factor_width)
    outer = jnp.einsum(
        "esa,esb->eab",
        grouped[..., factor_width:],
        grouped[..., :factor_width],
        precision=lax.Precision.HIGHEST,
    ) / math.sqrt(length)
    return outer.reshape(examples, factor_width * factor_width).astype(jnp.bfloat16)


def local(train_inputs, train_grads, bench_inputs, bench_grads, answer_mask, factors, precond):
    factor = factors[0]
    factor_width = factor.shape[1] // 2
    length = train_inputs.shape[2]
    masked = bench_grads[0] * answer_mask.astype(jnp.bfloat16)[:, :, None]
    train_rows = project(train_inputs[0], train_grads[0], factor)
    bench_rows = project(bench_inputs[0], masked, factor)
    tensor_count = lax.axis_size("tensor")
    train_each = train_inputs.shape[1] // tensor_count
    bench_each = bench_inputs.shape[1] // tensor_count
    row_width = train_rows.shape[1]
    blocks = jnp.concatenate(
        [
            train_rows.reshape(tensor_count, train_each * length, row_width),
            bench_rows.reshape(tensor_count, bench_each * length, row_width),
        ],
        axis=1,
    ).reshape(-1, row_width)
    share_rows = blocks.shape[0] // tensor_count
    summed = lax.psum(blocks, "tensor")
    own_rows = lax.dynamic_slice_in_dim(
        summed, lax.axis_index("tensor") * share_rows, share_rows, 0
    )
    train_feats = outer_features(own_rows[: train_each * length], train_each, length, factor_width)
    bench_feats = outer_features(own_rows[train_each * length :], bench_each, length, factor_width)
    columns = precond[0]
    pre_cols = jnp.dot(
        lax.all_gather(bench_feats, ("dp", "tensor"), axis=0, tiled=True),
        columns,
        preferred_element_type=jnp.float32,
    ).astype(jnp.bfloat16)
    layer_total = lax.axis_size("layer") * train_inputs.shape[0]
    score_scale = 1.0 / math.sqrt(factor_width * factor_width * layer_total)
    whole_pre = lax.all_gather(pre_cols, ("dp", "tensor"), axis=1, tiled=True)
    partial_value = jnp.einsum(
        "ek,jk->ej", train_feats, whole_pre, preferred_element_type=jnp.float32
    )
    scores = lax.psum_scatter(partial_value, "layer", scatter_dimension=0, tiled=True)
    return scores * score_scale


def fused_kernel(
    dims,
    ti, tg, bi, bg, mask, fac, pre,
    out,
    bench_v, train_v, fac_v, mask_v, pre_v,
    bench_part, bench_recv, train_part, train_recv,
    feats, train_f, t_send, t_all, partial_v, score_recv,
    load_sem, swap_send, swap_recv, feat_send, feat_recv, fwd_send,
    t_send_sem, t_recv_sem, score_send, score_recv_sem,
):
    n_dp, chunks, scale = dims
    f32, bf16 = jnp.float32, jnp.bfloat16
    z, x, layer = lax.axis_index("dp"), lax.axis_index("tensor"), lax.axis_index("layer")
    other = 1 - x
    slots = 2 * n_dp
    me = z * 2 + x
    bench_rows = bench_v.shape[2]
    train_rows = train_v.shape[2]
    length = mask.shape[1]
    width = 64
    chunk_width = feats.shape[3]
    blocks_per_chunk = chunk_width // 128
    columns = pre_v.shape[1]

    def load(source, target, index):
        return pltpu.make_async_copy(source, target, load_sem.at[index])

    def half(ref, position, rows):
        return ref.at[pl.ds(pl.multiple_of(position * rows, rows), rows), :]

    fac_load = load(fac, fac_v, 0)
    mask_load = load(mask, mask_v, 1)
    bench_loads = [
        load(half(ref, at, bench_rows), bench_v.at[h, i], 2 + 2 * h + i)
        for h, at in enumerate((other, x)) for i, ref in enumerate((bi, bg))
    ]
    train_loads = [
        load(half(ref, at, train_rows), train_v.at[h, i], 6 + 2 * h + i)
        for h, at in enumerate((other, x)) for i, ref in enumerate((ti, tg))
    ]
    pre_load = load(pre, pre_v, 10)
    fac_load.start()
    for one in bench_loads:
        one.start()
    mask_load.start()
    for one in train_loads:
        one.start()
    pre_load.start()

    steps = [(dz, dx) for dz in range(n_dp) for dx in range(2)]
    barrier = pltpu.get_barrier_semaphore()
    for dz, dx in steps:
        for dl in range(2):
            if dz or dx or dl:
                pl.semaphore_signal(
                    barrier, inc=1,
                    device_id={"dp": lax.rem(z + dz, n_dp), "tensor": lax.rem(x + dx, 2), "layer": lax.rem(layer + dl, 2)},
                    device_id_type=MESH,
                )

    def project(ref, rows):
        both = jnp.dot(
            ref[...].reshape(2 * rows, ref.shape[2]), fac_v[...], preferred_element_type=f32
        )
        lane = lax.broadcasted_iota(jnp.int32, (rows, 128), 1)
        return jnp.where(lane < width, both[:rows], both[rows:])

    bench_swap = pltpu.make_async_remote_copy(
        bench_part.at[0], bench_recv, swap_send.at[0], swap_recv.at[0],
        device_id={"tensor": other}, device_id_type=MESH,
    )
    train_swap = pltpu.make_async_remote_copy(
        train_part.at[0], train_recv, swap_send.at[1], swap_recv.at[1],
        device_id={"tensor": other}, device_id_type=MESH,
    )

    fac_load.wait()
    bench_loads[0].wait()
    bench_loads[1].wait()
    bench_part[0] = project(bench_v.at[0], bench_rows)
    pl.semaphore_wait(barrier, 4 * n_dp - 1)
    bench_swap.start()
    bench_loads[2].wait()
    bench_loads[3].wait()
    bench_part[1] = project(bench_v.at[1], bench_rows)
    train_loads[0].wait()
    train_loads[1].wait()
    train_part[0] = project(train_v.at[0], train_rows)
    train_swap.start()

    lane = lax.broadcasted_iota(jnp.int32, (8, 128), 1)

    def token_rows(own, recv, base):
        rows = []
        for t in range(length):
            window = pl.ds(base + t, 8, stride=length)
            rows.append(own[window, :] + recv[window, :])
        return rows

    def doubled(row):
        return jnp.where(lane < width, row, pltpu.roll(row, width, 1))

    def outer_block(firsts, seconds, block):
        index = width + 2 * block + jnp.where(lane < width, 0, 1)
        total = None
        for first, second in zip(firsts, seconds):
            term = jnp.take_along_axis(first, index, axis=1, mode="promise_in_bounds") * second
            total = term if total is None else total + term
        return total * (1.0 / math.sqrt(length))

    mask_load.wait()
    bench_swap.wait_recv()
    keep = mask_v[pl.ds(pl.multiple_of(x * 8, 8), 8), :].astype(f32)
    rows = token_rows(bench_part.at[1], bench_recv, 0)
    seconds = [doubled(row) for row in rows]
    firsts = [row * keep[:, t : t + 1] for t, row in enumerate(rows)]

    def feat_copy(c, slot, send_sem, device_id):
        return pltpu.make_async_remote_copy(
            feats.at[c, slot], feats.at[c, slot], send_sem, feat_recv.at[c, slot],
            device_id=device_id, device_id_type=MESH,
        )

    sent = []
    for c in range(chunks):
        def bench_block(k, carry, c=c):
            value = outer_block(firsts, seconds, c * blocks_per_chunk + k)
            feats[c, me, :, pl.ds(pl.multiple_of(k * 128, 128), 128)] = value.astype(bf16)
            return carry

        lax.fori_loop(0, blocks_per_chunk, bench_block, 0)
        for dz in range(1, n_dp):
            sent.append(feat_copy(c, me, feat_send.at[c, dz], {"dp": lax.rem(z + dz, n_dp)}))
        sent.append(feat_copy(c, me, feat_send.at[c, 0], {"tensor": other}))
        for one in sent[-n_dp:]:
            one.start()

    train_loads[2].wait()
    train_loads[3].wait()
    train_part[1] = project(train_v.at[1], train_rows)

    def forward(c):
        for dz in range(1, n_dp):
            slot = lax.rem(z + n_dp - dz, n_dp) * 2 + x
            one = feat_copy(c, slot, fwd_send.at[c, dz], {"tensor": other})
            one.wait_recv()
            one.start()
            sent.append(one)

    forward(0)
    forward(1)

    train_swap.wait_recv()
    per_slot = columns // 128
    groups_of_8 = train_f.shape[1] // 8
    for part in range(groups_of_8):
        rows = token_rows(train_part.at[1], train_recv, part * 8 * length)
        seconds_t = [doubled(row) for row in rows]

        def train_block(block, carry, rows=rows, seconds_t=seconds_t, part=part):
            train_f[block, part * 8 : part * 8 + 8, :] = outer_block(rows, seconds_t, block)
            return carry

        lax.fori_loop(0, slots * per_slot, train_block, 0)

    def t_copy(r, dz, dx):
        target = lax.rem(z + dz, n_dp) * 2 + lax.rem(x + dx, 2)
        return pltpu.make_async_remote_copy(
            t_send.at[target], t_all.at[r], t_send_sem.at[r], t_recv_sem.at[r],
            device_id={"dp": lax.rem(z + dz, n_dp), "tensor": lax.rem(x + dx, 2)}, device_id_type=MESH,
        )

    def pack(slot, carry):
        for k in range(per_slot):
            t_send[slot, :, k * 128 : (k + 1) * 128] = train_f[slot * per_slot + k].astype(bf16)
        return carry

    lax.fori_loop(0, slots, pack, 0)
    t_copies = [t_copy(r, dz, dx) for r, (dz, dx) in enumerate(steps) if r]
    for one in t_copies:
        one.start()
    t_all[0] = t_send[me]

    for c in range(2, chunks):
        forward(c)

    pre_load.wait()
    total = None
    for c in range(chunks):
        for zz in range(n_dp):
            slot = zz * 2 + other
            feat_copy(c, slot, feat_send.at[c, 0], {"tensor": other}).wait_recv()
        left = feats[c].astype(f32).reshape(slots * 8, chunk_width).astype(bf16)
        term = jnp.dot(
            left, pre_v[c * chunk_width : (c + 1) * chunk_width, :], preferred_element_type=f32
        )
        total = term if total is None else total + term
    bench_pre = jnp.concatenate([total, jnp.zeros((128 - slots * 8, columns), f32)], axis=0).astype(bf16)

    for one in t_copies:
        one.wait_recv()
    examples = t_all.shape[1]
    scores = lax.dot_general(
        t_all[...].reshape(slots * examples, columns), bench_pre,
        (((1,), (1,)), ((), ())), preferred_element_type=f32,
    )
    partial_v[...] = scores.reshape(slots, 2, 8, 128)
    score_copies = []
    for r, (dz, dx) in enumerate(steps):
        for dl in range(2):
            if r or dl:
                score_copies.append(
                    pltpu.make_async_remote_copy(
                        partial_v.at[r, lax.rem(layer + dl, 2)], score_recv.at[2 * r + dl],
                        score_send.at[2 * r + dl], score_recv_sem.at[2 * r + dl],
                        device_id={
                            "dp": lax.rem(z + n_dp - dz, n_dp),
                            "tensor": lax.rem(x + dx, 2),
                            "layer": lax.rem(layer + dl, 2),
                        },
                        device_id_type=MESH,
                    )
                )
    for one in score_copies:
        one.start()
    result = partial_v[0, layer]
    for index, one in enumerate(score_copies):
        one.wait_recv()
        result = result + score_recv[index + 1]
    out[...] = result[:, : out.shape[1]] * scale

    bench_swap.wait_send()
    train_swap.wait_send()
    for one in sent + t_copies + score_copies:
        one.wait_send()


def fused(train_inputs, train_grads, bench_inputs, bench_grads, answer_mask, factors, precond):
    f32, bf16 = jnp.float32, jnp.bfloat16
    _, train, length, shard = train_inputs.shape
    bench = bench_inputs.shape[1]
    n_dp = lax.axis_size("dp")
    slots = 2 * n_dp
    features, columns = precond.shape[1:]
    chunks = 4
    scale = 1.0 / math.sqrt(features * lax.axis_size("layer"))
    train_rows, bench_rows = train * length // 2, bench * length // 2
    dma = pltpu.SemaphoreType.DMA
    anywhere = pl.BlockSpec(memory_space=pl.ANY)
    return pl.pallas_call(
        functools.partial(fused_kernel, (n_dp, chunks, scale)),
        out_shape=jax.ShapeDtypeStruct((8, slots * 8), f32),
        in_specs=[anywhere] * 7,
        out_specs=pl.BlockSpec(memory_space=pltpu.VMEM),
        scratch_shapes=[
            pltpu.VMEM((2, 2, bench_rows, shard), bf16),
            pltpu.VMEM((2, 2, train_rows, shard), bf16),
            pltpu.VMEM((shard, 128), bf16),
            pltpu.VMEM((bench, length), jnp.int32),
            pltpu.VMEM((features, columns), bf16),
            pltpu.VMEM((2, bench_rows, 128), f32),
            pltpu.VMEM((bench_rows, 128), f32),
            pltpu.VMEM((2, train_rows, 128), f32),
            pltpu.VMEM((train_rows, 128), f32),
            pltpu.VMEM((chunks, slots, 8, features // chunks), bf16),
            pltpu.VMEM((features // 128, train // 2, 128), f32),
            pltpu.VMEM((slots, train // 2, columns), bf16),
            pltpu.VMEM((slots, train // 2, columns), bf16),
            pltpu.VMEM((slots, 2, 8, 128), f32),
            pltpu.VMEM((2 * slots, 8, 128), f32),
            dma((11,)),
            dma((2,)),
            dma((2,)),
            dma((chunks, n_dp)),
            dma((chunks, slots)),
            dma((chunks, n_dp)),
            dma((slots,)),
            dma((slots,)),
            dma((2 * slots,)),
            dma((2 * slots,)),
        ],
        compiler_params=pltpu.CompilerParams(
            collective_id=0, has_side_effects=True, vmem_limit_bytes=56 * 1024 * 1024
        ),
    )(
        train_inputs.reshape(train * length, shard),
        train_grads.reshape(train * length, shard),
        bench_inputs.reshape(bench * length, shard),
        bench_grads.reshape(bench * length, shard),
        answer_mask,
        factors[0],
        precond[0],
    )


def fits(shapes, sizes):
    train, bench, length, shard, half_width, features, columns, layers = shapes
    n_dp, n_tensor, n_layer = sizes
    return (
        n_tensor == 2 and n_layer == 2 and layers == 1 and half_width == 64 and length == 16
        and bench == 16 and train == 32 and n_dp * 16 <= 128
        and shard % 256 == 0 and columns % 128 == 0 and features == 4096
        and features == 2 * n_dp * columns
    )


def local_any(*args):
    train_inputs, _, bench_inputs, _, _, factors, precond = args
    shapes = (
        train_inputs.shape[1], bench_inputs.shape[1], train_inputs.shape[2], train_inputs.shape[3],
        factors.shape[2] // 2, precond.shape[1], precond.shape[2], train_inputs.shape[0],
    )
    sizes = tuple(lax.axis_size(name) for name in ("dp", "tensor", "layer"))
    return fused(*args) if fits(shapes, sizes) else local(*args)


def solution(mesh):
    placed = (
        P("layer", ("groups", "dp"), None, "tensor"),
        P("layer", ("groups", "dp"), None, "tensor"),
        P("layer", ("groups", "dp"), None, "tensor"),
        P("layer", ("groups", "dp"), None, "tensor"),
        P(("groups", "dp"), None),
        P("layer", "tensor", None),
        P("layer", None, ("dp", "tensor")),
    )
    return jax.shard_map(
        local_any,
        mesh=mesh,
        in_specs=placed,
        out_specs=P(("groups", "dp", "tensor", "layer"), None),
        check_vma=False,
    )
```

```python
import functools
import math

import jax
import jax.numpy as jnp
from jax import lax
from jax.experimental import pallas as pl
from jax.experimental.pallas import tpu as pltpu
from jax.sharding import PartitionSpec as P

MESH = pl.DeviceIdType.MESH


def project(inputs_here, grads_here, factor):
    examples, length, shard_width = inputs_here.shape
    factor_width = factor.shape[1] // 2
    in_proj = jnp.dot(
        inputs_here.reshape(examples * length, shard_width),
        factor[:, :factor_width],
        preferred_element_type=jnp.float32,
    )
    out_proj = jnp.dot(
        grads_here.reshape(examples * length, shard_width),
        factor[:, factor_width:],
        preferred_element_type=jnp.float32,
    )
    return jnp.concatenate([in_proj, out_proj], axis=1)


def outer_features(token_rows, examples, length, factor_width):
    grouped = token_rows.reshape(examples, length, 2 * factor_width)
    outer = jnp.einsum(
        "esa,esb->eab",
        grouped[..., factor_width:],
        grouped[..., :factor_width],
        precision=lax.Precision.HIGHEST,
    ) / math.sqrt(length)
    return outer.reshape(examples, factor_width * factor_width).astype(jnp.bfloat16)


def local(train_inputs, train_grads, bench_inputs, bench_grads, answer_mask, factors, precond):
    factor = factors[0]
    factor_width = factor.shape[1] // 2
    length = train_inputs.shape[2]
    masked = bench_grads[0] * answer_mask.astype(jnp.bfloat16)[:, :, None]
    train_rows = project(train_inputs[0], train_grads[0], factor)
    bench_rows = project(bench_inputs[0], masked, factor)
    tensor_count = lax.axis_size("tensor")
    train_each = train_inputs.shape[1] // tensor_count
    bench_each = bench_inputs.shape[1] // tensor_count
    row_width = train_rows.shape[1]
    blocks = jnp.concatenate(
        [
            train_rows.reshape(tensor_count, train_each * length, row_width),
            bench_rows.reshape(tensor_count, bench_each * length, row_width),
        ],
        axis=1,
    ).reshape(-1, row_width)
    share_rows = blocks.shape[0] // tensor_count
    summed = lax.psum(blocks, "tensor")
    own_rows = lax.dynamic_slice_in_dim(
        summed, lax.axis_index("tensor") * share_rows, share_rows, 0
    )
    train_feats = outer_features(own_rows[: train_each * length], train_each, length, factor_width)
    bench_feats = outer_features(own_rows[train_each * length :], bench_each, length, factor_width)
    columns = precond[0]
    pre_cols = jnp.dot(
        lax.all_gather(bench_feats, ("dp", "tensor"), axis=0, tiled=True),
        columns,
        preferred_element_type=jnp.float32,
    ).astype(jnp.bfloat16)
    layer_total = lax.axis_size("layer") * train_inputs.shape[0]
    score_scale = 1.0 / math.sqrt(factor_width * factor_width * layer_total)
    whole_pre = lax.all_gather(pre_cols, ("dp", "tensor"), axis=1, tiled=True)
    partial_value = jnp.einsum(
        "ek,jk->ej", train_feats, whole_pre, preferred_element_type=jnp.float32
    )
    scores = lax.psum_scatter(partial_value, "layer", scatter_dimension=0, tiled=True)
    return scores * score_scale


def fused_kernel(
    dims,
    ti, tg, bi, bg, mask, fac, pre,
    out,
    bench_v, train_v, fac_v, mask_v, pre_v,
    bench_part, bench_recv, train_part, train_recv,
    feats, spread_v, t_send, t_all, partial_v, score_recv,
    load_sem, swap_send, swap_recv, feat_send, feat_recv, fwd_send,
    t_send_sem, t_recv_sem, score_send, score_recv_sem,
):
    n_dp, chunks, scale = dims
    f32, bf16 = jnp.float32, jnp.bfloat16
    z, x, layer = lax.axis_index("dp"), lax.axis_index("tensor"), lax.axis_index("layer")
    other = 1 - x
    slots = 2 * n_dp
    me = z * 2 + x
    bench_rows = bench_v.shape[2]
    train_rows = train_v.shape[2]
    length = mask.shape[1]
    width = 64
    chunk_width = feats.shape[3]
    span = 512
    columns = pre_v.shape[1]

    def load(source, target, index):
        return pltpu.make_async_copy(source, target, load_sem.at[index])

    def half(ref, position, rows):
        return ref.at[pl.ds(pl.multiple_of(position * rows, rows), rows), :]

    fac_load = load(fac, fac_v, 0)
    mask_load = load(mask, mask_v, 1)
    bench_loads = [
        load(half(ref, at, bench_rows), bench_v.at[h, i], 2 + 2 * h + i)
        for h, at in enumerate((other, x)) for i, ref in enumerate((bi, bg))
    ]
    train_loads = [
        load(half(ref, at, train_rows), train_v.at[h, i], 6 + 2 * h + i)
        for h, at in enumerate((other, x)) for i, ref in enumerate((ti, tg))
    ]
    pre_load = load(pre, pre_v, 10)
    fac_load.start()
    for one in bench_loads:
        one.start()
    mask_load.start()
    for one in train_loads:
        one.start()
    pre_load.start()

    steps = [(dz, dx) for dz in range(n_dp) for dx in range(2)]
    barrier = pltpu.get_barrier_semaphore()
    for dz, dx in steps:
        for dl in range(2):
            if dz or dx or dl:
                pl.semaphore_signal(
                    barrier, inc=1,
                    device_id={"dp": lax.rem(z + dz, n_dp), "tensor": lax.rem(x + dx, 2), "layer": lax.rem(layer + dl, 2)},
                    device_id_type=MESH,
                )

    def build(k, carry):
        row = lax.broadcasted_iota(jnp.int32, (256, 256), 0)
        column = lax.broadcasted_iota(jnp.int32, (256, 256), 1) + k * 256
        hit = (row % 128) * width - width * width == column - column % width
        spread_v[:, pl.ds(pl.multiple_of(k * 256, 256), 256)] = jnp.where(hit, 1.0, 0.0).astype(bf16)
        return carry

    lax.fori_loop(0, spread_v.shape[1] // 256, build, 0)

    def project(ref, rows):
        both = jnp.dot(
            ref[...].reshape(2 * rows, ref.shape[2]), fac_v[...], preferred_element_type=f32
        )
        lane = lax.broadcasted_iota(jnp.int32, (rows, 128), 1)
        return jnp.where(lane < width, both[:rows], both[rows:])

    bench_swap = pltpu.make_async_remote_copy(
        bench_part.at[0], bench_recv, swap_send.at[0], swap_recv.at[0],
        device_id={"tensor": other}, device_id_type=MESH,
    )
    train_swap = pltpu.make_async_remote_copy(
        train_part.at[0], train_recv, swap_send.at[1], swap_recv.at[1],
        device_id={"tensor": other}, device_id_type=MESH,
    )

    fac_load.wait()
    bench_loads[0].wait()
    bench_loads[1].wait()
    bench_part[0] = project(bench_v.at[0], bench_rows)
    pl.semaphore_wait(barrier, 4 * n_dp - 1)
    bench_swap.start()
    bench_loads[2].wait()
    bench_loads[3].wait()
    bench_part[1] = project(bench_v.at[1], bench_rows)
    train_loads[0].wait()
    train_loads[1].wait()
    train_part[0] = project(train_v.at[0], train_rows)
    train_swap.start()

    lane = lax.broadcasted_iota(jnp.int32, (8, 128), 1)

    def token_rows(own, recv, base):
        rows = []
        for t in range(length):
            window = pl.ds(base + t, 8, stride=length)
            rows.append(own[window, :] + recv[window, :])
        return rows

    def doubled(row):
        return jnp.where(lane < width, row, pltpu.roll(row, width, 1))

    def split(rows):
        whole = jnp.concatenate(rows, axis=0)
        high = whole.astype(bf16)
        low = (whole - high.astype(f32)).astype(bf16)
        return jnp.concatenate([high, low], axis=1)

    def outer(parts, seconds, start, span):
        spread = jnp.dot(
            parts, spread_v[:, pl.ds(pl.multiple_of(start, span), span)], preferred_element_type=f32
        )
        values = []
        for first in range(0, len(seconds), length):
            lanes = []
            for j in range(0, span, 128):
                total = None
                for t in range(first, first + length):
                    term = spread[t * 8 : t * 8 + 8, j : j + 128] * seconds[t]
                    total = term if total is None else total + term
                lanes.append(total)
            values.append(jnp.concatenate(lanes, axis=1))
        return jnp.concatenate(values, axis=0) * (1.0 / math.sqrt(length))

    mask_load.wait()
    bench_swap.wait_recv()
    keep = mask_v[pl.ds(pl.multiple_of(x * 8, 8), 8), :].astype(f32)
    rows = token_rows(bench_part.at[1], bench_recv, 0)
    seconds = [doubled(row) for row in rows]
    bench_split = split([row * keep[:, t : t + 1] for t, row in enumerate(rows)])

    def feat_copy(c, slot, send_sem, device_id):
        return pltpu.make_async_remote_copy(
            feats.at[c, slot], feats.at[c, slot], send_sem, feat_recv.at[c, slot],
            device_id=device_id, device_id_type=MESH,
        )

    sent = []
    for c in range(chunks):
        def bench_block(k, carry, c=c):
            value = outer(bench_split, seconds, c * chunk_width + k * span, span)
            feats[c, me, :, pl.ds(pl.multiple_of(k * span, span), span)] = value.astype(bf16)
            return carry

        lax.fori_loop(0, chunk_width // span, bench_block, 0)
        for dz in range(1, n_dp):
            sent.append(feat_copy(c, me, feat_send.at[c, dz], {"dp": lax.rem(z + dz, n_dp)}))
        sent.append(feat_copy(c, me, feat_send.at[c, 0], {"tensor": other}))
        for one in sent[-n_dp:]:
            one.start()

    train_loads[2].wait()
    train_loads[3].wait()
    train_part[1] = project(train_v.at[1], train_rows)

    def forward(c):
        for dz in range(1, n_dp):
            slot = lax.rem(z + n_dp - dz, n_dp) * 2 + x
            one = feat_copy(c, slot, fwd_send.at[c, dz], {"tensor": other})
            one.wait_recv()
            one.start()
            sent.append(one)

    forward(0)
    forward(1)

    train_swap.wait_recv()
    rows = []
    for part in range(0, t_send.shape[1], 8):
        rows += token_rows(train_part.at[1], train_recv, part * length)
    train_seconds = [doubled(row) for row in rows]
    train_split = split(rows)

    def train_block(slot, carry):
        t_send[slot] = outer(train_split, train_seconds, slot * columns, columns).astype(bf16)
        return carry

    lax.fori_loop(0, slots, train_block, 0)

    def t_copy(r, dz, dx):
        target = lax.rem(z + dz, n_dp) * 2 + lax.rem(x + dx, 2)
        return pltpu.make_async_remote_copy(
            t_send.at[target], t_all.at[r], t_send_sem.at[r], t_recv_sem.at[r],
            device_id={"dp": lax.rem(z + dz, n_dp), "tensor": lax.rem(x + dx, 2)}, device_id_type=MESH,
        )

    t_copies = [t_copy(r, dz, dx) for r, (dz, dx) in enumerate(steps) if r]
    for one in t_copies:
        one.start()
    t_all[0] = t_send[me]

    for c in range(2, chunks):
        forward(c)

    pre_load.wait()
    total = None
    for c in range(chunks):
        for zz in range(n_dp):
            slot = zz * 2 + other
            feat_copy(c, slot, feat_send.at[c, 0], {"tensor": other}).wait_recv()
        left = feats[c].astype(f32).reshape(slots * 8, chunk_width).astype(bf16)
        term = jnp.dot(
            left, pre_v[c * chunk_width : (c + 1) * chunk_width, :], preferred_element_type=f32
        )
        total = term if total is None else total + term
    bench_pre = jnp.concatenate([total, jnp.zeros((128 - slots * 8, columns), f32)], axis=0).astype(bf16)

    for one in t_copies:
        one.wait_recv()
    examples = t_all.shape[1]
    scores = lax.dot_general(
        t_all[...].reshape(slots * examples, columns), bench_pre,
        (((1,), (1,)), ((), ())), preferred_element_type=f32,
    )
    partial_v[...] = scores.reshape(slots, 2, 8, 128)
    score_copies = []
    for r, (dz, dx) in enumerate(steps):
        for dl in range(2):
            if r or dl:
                score_copies.append(
                    pltpu.make_async_remote_copy(
                        partial_v.at[r, lax.rem(layer + dl, 2)], score_recv.at[2 * r + dl],
                        score_send.at[2 * r + dl], score_recv_sem.at[2 * r + dl],
                        device_id={
                            "dp": lax.rem(z + n_dp - dz, n_dp),
                            "tensor": lax.rem(x + dx, 2),
                            "layer": lax.rem(layer + dl, 2),
                        },
                        device_id_type=MESH,
                    )
                )
    for one in score_copies:
        one.start()
    result = partial_v[0, layer]
    for index, one in enumerate(score_copies):
        one.wait_recv()
        result = result + score_recv[index + 1]
    out[...] = result[:, : out.shape[1]] * scale

    bench_swap.wait_send()
    train_swap.wait_send()
    for one in sent + t_copies + score_copies:
        one.wait_send()


def fused(train_inputs, train_grads, bench_inputs, bench_grads, answer_mask, factors, precond):
    f32, bf16 = jnp.float32, jnp.bfloat16
    _, train, length, shard = train_inputs.shape
    bench = bench_inputs.shape[1]
    n_dp = lax.axis_size("dp")
    slots = 2 * n_dp
    features, columns = precond.shape[1:]
    chunks = 4
    scale = 1.0 / math.sqrt(features * lax.axis_size("layer"))
    train_rows, bench_rows = train * length // 2, bench * length // 2
    dma = pltpu.SemaphoreType.DMA
    anywhere = pl.BlockSpec(memory_space=pl.ANY)
    return pl.pallas_call(
        functools.partial(fused_kernel, (n_dp, chunks, scale)),
        out_shape=jax.ShapeDtypeStruct((8, slots * 8), f32),
        in_specs=[anywhere] * 7,
        out_specs=pl.BlockSpec(memory_space=pltpu.VMEM),
        scratch_shapes=[
            pltpu.VMEM((2, 2, bench_rows, shard), bf16),
            pltpu.VMEM((2, 2, train_rows, shard), bf16),
            pltpu.VMEM((shard, 128), bf16),
            pltpu.VMEM((bench, length), jnp.int32),
            pltpu.VMEM((features, columns), bf16),
            pltpu.VMEM((2, bench_rows, 128), f32),
            pltpu.VMEM((bench_rows, 128), f32),
            pltpu.VMEM((2, train_rows, 128), f32),
            pltpu.VMEM((train_rows, 128), f32),
            pltpu.VMEM((chunks, slots, 8, features // chunks), bf16),
            pltpu.VMEM((256, features), bf16),
            pltpu.VMEM((slots, train // 2, columns), bf16),
            pltpu.VMEM((slots, train // 2, columns), bf16),
            pltpu.VMEM((slots, 2, 8, 128), f32),
            pltpu.VMEM((2 * slots, 8, 128), f32),
            dma((11,)),
            dma((2,)),
            dma((2,)),
            dma((chunks, n_dp)),
            dma((chunks, slots)),
            dma((chunks, n_dp)),
            dma((slots,)),
            dma((slots,)),
            dma((2 * slots,)),
            dma((2 * slots,)),
        ],
        compiler_params=pltpu.CompilerParams(
            collective_id=0, has_side_effects=True, vmem_limit_bytes=56 * 1024 * 1024
        ),
    )(
        train_inputs.reshape(train * length, shard),
        train_grads.reshape(train * length, shard),
        bench_inputs.reshape(bench * length, shard),
        bench_grads.reshape(bench * length, shard),
        answer_mask,
        factors[0],
        precond[0],
    )


def fits(shapes, sizes):
    train, bench, length, shard, half_width, features, columns, layers = shapes
    n_dp, n_tensor, n_layer = sizes
    return (
        n_tensor == 2 and n_layer == 2 and layers == 1 and half_width == 64 and length == 16
        and bench == 16 and train == 32 and n_dp * 16 <= 128
        and shard % 256 == 0 and columns % 128 == 0 and features == 4096
        and features == 2 * n_dp * columns
    )


def local_any(*args):
    train_inputs, _, bench_inputs, _, _, factors, precond = args
    shapes = (
        train_inputs.shape[1], bench_inputs.shape[1], train_inputs.shape[2], train_inputs.shape[3],
        factors.shape[2] // 2, precond.shape[1], precond.shape[2], train_inputs.shape[0],
    )
    sizes = tuple(lax.axis_size(name) for name in ("dp", "tensor", "layer"))
    return fused(*args) if fits(shapes, sizes) else local(*args)


def solution(mesh):
    placed = (
        P("layer", ("groups", "dp"), None, "tensor"),
        P("layer", ("groups", "dp"), None, "tensor"),
        P("layer", ("groups", "dp"), None, "tensor"),
        P("layer", ("groups", "dp"), None, "tensor"),
        P(("groups", "dp"), None),
        P("layer", "tensor", None),
        P("layer", None, ("dp", "tensor")),
    )
    return jax.shard_map(
        local_any,
        mesh=mesh,
        in_specs=placed,
        out_specs=P(("groups", "dp", "tensor", "layer"), None),
        check_vma=False,
    )
```

```python
import functools
import math

import jax
import jax.numpy as jnp
from jax import lax
from jax.experimental import pallas as pl
from jax.experimental.pallas import tpu as pltpu
from jax.sharding import PartitionSpec as P

MESH = pl.DeviceIdType.MESH


def project(inputs_here, grads_here, factor):
    examples, length, shard_width = inputs_here.shape
    factor_width = factor.shape[1] // 2
    in_proj = jnp.dot(
        inputs_here.reshape(examples * length, shard_width),
        factor[:, :factor_width],
        preferred_element_type=jnp.float32,
    )
    out_proj = jnp.dot(
        grads_here.reshape(examples * length, shard_width),
        factor[:, factor_width:],
        preferred_element_type=jnp.float32,
    )
    return jnp.concatenate([in_proj, out_proj], axis=1)


def outer_features(token_rows, examples, length, factor_width):
    grouped = token_rows.reshape(examples, length, 2 * factor_width)
    outer = jnp.einsum(
        "esa,esb->eab",
        grouped[..., factor_width:],
        grouped[..., :factor_width],
        precision=lax.Precision.HIGHEST,
    ) / math.sqrt(length)
    return outer.reshape(examples, factor_width * factor_width).astype(jnp.bfloat16)


def local(train_inputs, train_grads, bench_inputs, bench_grads, answer_mask, factors, precond):
    factor = factors[0]
    factor_width = factor.shape[1] // 2
    length = train_inputs.shape[2]
    masked = bench_grads[0] * answer_mask.astype(jnp.bfloat16)[:, :, None]
    train_rows = project(train_inputs[0], train_grads[0], factor)
    bench_rows = project(bench_inputs[0], masked, factor)
    tensor_count = lax.axis_size("tensor")
    train_each = train_inputs.shape[1] // tensor_count
    bench_each = bench_inputs.shape[1] // tensor_count
    row_width = train_rows.shape[1]
    blocks = jnp.concatenate(
        [
            train_rows.reshape(tensor_count, train_each * length, row_width),
            bench_rows.reshape(tensor_count, bench_each * length, row_width),
        ],
        axis=1,
    ).reshape(-1, row_width)
    share_rows = blocks.shape[0] // tensor_count
    summed = lax.psum(blocks, "tensor")
    own_rows = lax.dynamic_slice_in_dim(
        summed, lax.axis_index("tensor") * share_rows, share_rows, 0
    )
    train_feats = outer_features(own_rows[: train_each * length], train_each, length, factor_width)
    bench_feats = outer_features(own_rows[train_each * length :], bench_each, length, factor_width)
    columns = precond[0]
    pre_cols = jnp.dot(
        lax.all_gather(bench_feats, ("dp", "tensor"), axis=0, tiled=True),
        columns,
        preferred_element_type=jnp.float32,
    ).astype(jnp.bfloat16)
    layer_total = lax.axis_size("layer") * train_inputs.shape[0]
    score_scale = 1.0 / math.sqrt(factor_width * factor_width * layer_total)
    whole_pre = lax.all_gather(pre_cols, ("dp", "tensor"), axis=1, tiled=True)
    partial_value = jnp.einsum(
        "ek,jk->ej", train_feats, whole_pre, preferred_element_type=jnp.float32
    )
    scores = lax.psum_scatter(partial_value, "layer", scatter_dimension=0, tiled=True)
    return scores * score_scale


def fused_kernel(
    dims,
    ti, tg, bi, bg, mask, fac, pre,
    out,
    bench_v, train_v, fac_v, mask_v, pre_v,
    bench_part, bench_recv, train_part, train_recv,
    feats, proj, spread_v, t_send, t_all, partial_v, both_v, pair_recv, score_recv,
    load_sem, swap_send, swap_recv, feat_send, feat_recv, fwd_send,
    t_send_sem, t_recv_sem, score_send, score_recv_sem,
):
    n_dp, scale = dims
    f32, bf16 = jnp.float32, jnp.bfloat16
    z, x, layer = lax.axis_index("dp"), lax.axis_index("tensor"), lax.axis_index("layer")
    other = 1 - x
    slots = 2 * n_dp
    me = z * 2 + x
    bench_rows = bench_v.shape[2]
    train_rows = train_v.shape[2]
    length = mask.shape[1]
    width = 64
    span = 512
    columns = pre_v.shape[1]

    def load(source, target, index):
        return pltpu.make_async_copy(source, target, load_sem.at[index])

    def half(ref, position, rows):
        return ref.at[pl.ds(pl.multiple_of(position * rows, rows), rows), :]

    fac_load = load(fac, fac_v, 0)
    mask_load = load(mask, mask_v, 1)
    bench_loads = [
        load(half(ref, at, bench_rows), bench_v.at[h, i], 2 + 2 * h + i)
        for h, at in enumerate((other, x)) for i, ref in enumerate((bi, bg))
    ]
    train_loads = [
        load(half(ref, at, train_rows), train_v.at[h, i], 6 + 2 * h + i)
        for h, at in enumerate((other, x)) for i, ref in enumerate((ti, tg))
    ]
    pre_load = load(pre, pre_v, 10)
    fac_load.start()
    for one in bench_loads:
        one.start()
    mask_load.start()
    for one in train_loads:
        one.start()
    pre_load.start()

    steps = [(dz, dx) for dz in range(n_dp) for dx in range(2)]
    barrier = pltpu.get_barrier_semaphore()
    partners = [
        {"dp": lax.rem(z + dz, n_dp), "tensor": lax.rem(x + dx, 2)} for dz, dx in steps if dz or dx
    ]
    partners.append({"layer": 1 - layer})
    for partner in partners:
        pl.semaphore_signal(barrier, inc=1, device_id=partner, device_id_type=MESH)

    def build(k, carry):
        row = lax.broadcasted_iota(jnp.int32, (256, 256), 0)
        column = lax.broadcasted_iota(jnp.int32, (256, 256), 1) + k * 256
        hit = (row % 128) * width - width * width == column - column % width
        spread_v[:, pl.ds(pl.multiple_of(k * 256, 256), 256)] = jnp.where(hit, 1.0, 0.0).astype(bf16)
        return carry

    lax.fori_loop(0, spread_v.shape[1] // 256, build, 0)

    def project(ref, rows):
        both = jnp.dot(
            ref[...].reshape(2 * rows, ref.shape[2]), fac_v[...], preferred_element_type=f32
        )
        lane = lax.broadcasted_iota(jnp.int32, (rows, 128), 1)
        return jnp.where(lane < width, both[:rows], both[rows:])

    bench_swap = pltpu.make_async_remote_copy(
        bench_part.at[0], bench_recv, swap_send.at[0], swap_recv.at[0],
        device_id={"tensor": other}, device_id_type=MESH,
    )
    train_swap = pltpu.make_async_remote_copy(
        train_part.at[0], train_recv, swap_send.at[1], swap_recv.at[1],
        device_id={"tensor": other}, device_id_type=MESH,
    )

    fac_load.wait()
    bench_loads[0].wait()
    bench_loads[1].wait()
    bench_part[0] = project(bench_v.at[0], bench_rows)
    pl.semaphore_wait(barrier, slots)
    bench_swap.start()
    bench_loads[2].wait()
    bench_loads[3].wait()
    bench_part[1] = project(bench_v.at[1], bench_rows)
    train_loads[0].wait()
    train_loads[1].wait()
    train_part[0] = project(train_v.at[0], train_rows)
    train_swap.start()

    lane = lax.broadcasted_iota(jnp.int32, (8, 128), 1)

    def token_rows(own, recv, base):
        rows = []
        for t in range(length):
            window = pl.ds(base + t, 8, stride=length)
            rows.append(own[window, :] + recv[window, :])
        return rows

    def doubled(row):
        return jnp.where(lane < width, row, pltpu.roll(row, width, 1))

    def split(rows):
        whole = jnp.concatenate(rows, axis=0)
        high = whole.astype(bf16)
        low = (whole - high.astype(f32)).astype(bf16)
        return jnp.concatenate([high, low], axis=1)

    def outer(parts, seconds, start, span):
        spread = jnp.dot(
            parts, spread_v[: parts.shape[1], pl.ds(pl.multiple_of(start, span), span)], preferred_element_type=f32
        )
        values = []
        for first in range(0, len(seconds), length):
            lanes = []
            for j in range(0, span, 128):
                total = None
                for t in range(first, first + length):
                    term = spread[t * 8 : t * 8 + 8, j : j + 128] * seconds[t]
                    total = term if total is None else total + term
                lanes.append(total)
            values.append(jnp.concatenate(lanes, axis=1))
        return jnp.concatenate(values, axis=0) * (1.0 / math.sqrt(length))

    mask_load.wait()
    bench_swap.wait_recv()
    keep = mask_v[pl.ds(pl.multiple_of(x * 8, 8), 8), :].astype(f32)
    rows = token_rows(bench_part.at[1], bench_recv, 0)
    seconds = [doubled(row) for row in rows]
    masked = [jnp.where(lane < width, row, row * keep[:, t : t + 1]) for t, row in enumerate(rows)]
    proj[me] = jnp.concatenate(masked, axis=0).astype(bf16)

    def proj_copy(slot, send_sem, device_id):
        return pltpu.make_async_remote_copy(
            proj.at[slot], proj.at[slot], send_sem, feat_recv.at[slot],
            device_id=device_id, device_id_type=MESH,
        )

    sent = [proj_copy(me, feat_send.at[dz], {"dp": lax.rem(z + dz, n_dp)}) for dz in range(1, n_dp)]
    sent.append(proj_copy(me, feat_send.at[0], {"tensor": other}))
    for one in sent:
        one.start()

    train_loads[2].wait()
    train_loads[3].wait()
    train_part[1] = project(train_v.at[1], train_rows)

    for dz in range(1, n_dp):
        one = proj_copy(lax.rem(z + n_dp - dz, n_dp) * 2 + x, fwd_send.at[dz], {"tensor": other})
        one.wait_recv()
        one.start()
        sent.append(one)

    train_swap.wait_recv()
    rows = []
    for part in range(0, t_send.shape[1], 8):
        rows += token_rows(train_part.at[1], train_recv, part * length)
    train_seconds = [doubled(row) for row in rows]
    train_split = split(rows)

    def train_block(slot, carry):
        t_send[slot] = outer(train_split, train_seconds, slot * columns, columns).astype(bf16)
        return carry

    lax.fori_loop(0, slots, train_block, 0, unroll=4)

    def t_copy(r, dz, dx):
        target = lax.rem(z + dz, n_dp) * 2 + lax.rem(x + dx, 2)
        return pltpu.make_async_remote_copy(
            t_send.at[target], t_all.at[r], t_send_sem.at[r], t_recv_sem.at[r],
            device_id={"dp": lax.rem(z + dz, n_dp), "tensor": lax.rem(x + dx, 2)}, device_id_type=MESH,
        )

    t_copies = [t_copy(r, dz, dx) for r, (dz, dx) in enumerate(steps) if r]
    for one in t_copies:
        one.start()
    t_all[0] = t_send[me]

    def bench_slot(slot):
        tokens = proj[slot]
        bench_seconds = [doubled(tokens[t * 8 : t * 8 + 8].astype(f32)) for t in range(length)]

        def bench_block(k, carry):
            start = pl.multiple_of(k * span, span)
            feats[slot, :, pl.ds(start, span)] = outer(tokens, bench_seconds, start, span)
            return carry

        lax.fori_loop(0, feats.shape[2] // span, bench_block, 0, unroll=True)

    def own_column(dz, carry):
        bench_slot(lax.rem(z + n_dp - dz, n_dp) * 2 + x)
        return carry

    lax.fori_loop(0, n_dp, own_column, 0)

    def other_column(dz, carry):
        slot = lax.rem(z + n_dp - dz, n_dp) * 2 + other
        proj_copy(slot, feat_send.at[0], {"tensor": other}).wait_recv()
        bench_slot(slot)
        return carry

    lax.fori_loop(0, n_dp, other_column, 0)

    pre_load.wait()
    total = jnp.dot(
        feats[...].reshape(slots * 8, feats.shape[2]).astype(bf16), pre_v[...], preferred_element_type=f32
    )
    bench_pre = jnp.concatenate([total, jnp.zeros((128 - slots * 8, columns), f32)], axis=0)
    pre_high = bench_pre.astype(bf16)
    pre_low = (bench_pre - pre_high.astype(f32)).astype(bf16)

    for one in t_copies:
        one.wait_recv()
    examples = t_all.shape[1]
    held = t_all[...].reshape(slots * examples, columns)
    along = (((1,), (1,)), ((), ()))
    scores = lax.dot_general(held, pre_high, along, preferred_element_type=f32)
    scores += lax.dot_general(held, pre_low, along, preferred_element_type=f32)
    scores = scores.reshape(slots, 2, 8, 128)
    for which in range(2):
        partial_v[which] = scores[:, which]
    pair = pltpu.make_async_remote_copy(
        partial_v.at[1 - layer], pair_recv, score_send.at[0], score_recv_sem.at[0],
        device_id={"layer": 1 - layer}, device_id_type=MESH,
    )
    pair.start()
    pair.wait_recv()
    both_v[...] = partial_v[layer] + pair_recv[...]
    score_copies = []
    for r, (dz, dx) in enumerate(steps):
        if r:
            score_copies.append(
                pltpu.make_async_remote_copy(
                    both_v.at[r], score_recv.at[r], score_send.at[r], score_recv_sem.at[r],
                    device_id={"dp": lax.rem(z + n_dp - dz, n_dp), "tensor": lax.rem(x + dx, 2)},
                    device_id_type=MESH,
                )
            )
    for one in score_copies:
        one.start()
    result = both_v[0]
    for index, one in enumerate(score_copies):
        one.wait_recv()
        result = result + score_recv[index + 1]
    out[...] = result[:, : out.shape[1]] * scale

    pair.wait_send()
    bench_swap.wait_send()
    train_swap.wait_send()
    for one in sent + t_copies + score_copies:
        one.wait_send()


def fused(train_inputs, train_grads, bench_inputs, bench_grads, answer_mask, factors, precond):
    f32, bf16 = jnp.float32, jnp.bfloat16
    _, train, length, shard = train_inputs.shape
    bench = bench_inputs.shape[1]
    n_dp = lax.axis_size("dp")
    slots = 2 * n_dp
    features, columns = precond.shape[1:]
    scale = 1.0 / math.sqrt(features * lax.axis_size("layer"))
    train_rows, bench_rows = train * length // 2, bench * length // 2
    dma = pltpu.SemaphoreType.DMA
    anywhere = pl.BlockSpec(memory_space=pl.ANY)
    return pl.pallas_call(
        functools.partial(fused_kernel, (n_dp, scale)),
        out_shape=jax.ShapeDtypeStruct((8, slots * 8), f32),
        in_specs=[anywhere] * 7,
        out_specs=pl.BlockSpec(memory_space=pltpu.VMEM),
        scratch_shapes=[
            pltpu.VMEM((2, 2, bench_rows, shard), bf16),
            pltpu.VMEM((2, 2, train_rows, shard), bf16),
            pltpu.VMEM((shard, 128), bf16),
            pltpu.VMEM((bench, length), jnp.int32),
            pltpu.VMEM((features, columns), bf16),
            pltpu.VMEM((2, bench_rows, 128), f32),
            pltpu.VMEM((bench_rows, 128), f32),
            pltpu.VMEM((2, train_rows, 128), f32),
            pltpu.VMEM((train_rows, 128), f32),
            pltpu.VMEM((slots, 8, features), f32),
            pltpu.VMEM((slots, bench_rows, 128), bf16),
            pltpu.VMEM((256, features), bf16),
            pltpu.VMEM((slots, train // 2, columns), bf16),
            pltpu.VMEM((slots, train // 2, columns), bf16),
            pltpu.VMEM((2, slots, 8, 128), f32),
            pltpu.VMEM((slots, 8, 128), f32),
            pltpu.VMEM((slots, 8, 128), f32),
            pltpu.VMEM((slots, 8, 128), f32),
            dma((11,)),
            dma((2,)),
            dma((2,)),
            dma((n_dp,)),
            dma((slots,)),
            dma((n_dp,)),
            dma((slots,)),
            dma((slots,)),
            dma((slots,)),
            dma((slots,)),
        ],
        compiler_params=pltpu.CompilerParams(
            collective_id=0, has_side_effects=True, vmem_limit_bytes=56 * 1024 * 1024
        ),
    )(
        train_inputs.reshape(train * length, shard),
        train_grads.reshape(train * length, shard),
        bench_inputs.reshape(bench * length, shard),
        bench_grads.reshape(bench * length, shard),
        answer_mask,
        factors[0],
        precond[0],
    )


def fits(shapes, sizes):
    train, bench, length, shard, half_width, features, columns, layers = shapes
    n_dp, n_tensor, n_layer = sizes
    return (
        n_tensor == 2 and n_layer == 2 and layers == 1 and half_width == 64 and length == 16
        and bench == 16 and train == 32 and n_dp * 16 <= 128
        and shard % 256 == 0 and columns % 128 == 0 and features == 4096
        and features == 2 * n_dp * columns
    )


def local_any(*args):
    train_inputs, _, bench_inputs, _, _, factors, precond = args
    shapes = (
        train_inputs.shape[1], bench_inputs.shape[1], train_inputs.shape[2], train_inputs.shape[3],
        factors.shape[2] // 2, precond.shape[1], precond.shape[2], train_inputs.shape[0],
    )
    sizes = tuple(lax.axis_size(name) for name in ("dp", "tensor", "layer"))
    return fused(*args) if fits(shapes, sizes) else local(*args)


def solution(mesh):
    placed = (
        P("layer", ("groups", "dp"), None, "tensor"),
        P("layer", ("groups", "dp"), None, "tensor"),
        P("layer", ("groups", "dp"), None, "tensor"),
        P("layer", ("groups", "dp"), None, "tensor"),
        P(("groups", "dp"), None),
        P("layer", "tensor", None),
        P("layer", None, ("dp", "tensor")),
    )
    return jax.shard_map(
        local_any,
        mesh=mesh,
        in_specs=placed,
        out_specs=P(("groups", "dp", "tensor", "layer"), None),
        check_vma=False,
    )
```

```python
import functools
import math

import jax
import jax.numpy as jnp
from jax import lax
from jax.experimental import pallas as pl
from jax.experimental.pallas import tpu as pltpu
from jax.sharding import PartitionSpec as P

MESH = pl.DeviceIdType.MESH


def project(inputs_here, grads_here, factor):
    examples, length, shard_width = inputs_here.shape
    factor_width = factor.shape[1] // 2
    in_proj = jnp.dot(
        inputs_here.reshape(examples * length, shard_width),
        factor[:, :factor_width],
        preferred_element_type=jnp.float32,
    )
    out_proj = jnp.dot(
        grads_here.reshape(examples * length, shard_width),
        factor[:, factor_width:],
        preferred_element_type=jnp.float32,
    )
    return jnp.concatenate([in_proj, out_proj], axis=1)


def outer_features(token_rows, examples, length, factor_width):
    grouped = token_rows.reshape(examples, length, 2 * factor_width)
    outer = jnp.einsum(
        "esa,esb->eab",
        grouped[..., factor_width:],
        grouped[..., :factor_width],
        precision=lax.Precision.HIGHEST,
    ) / math.sqrt(length)
    return outer.reshape(examples, factor_width * factor_width).astype(jnp.bfloat16)


def local(train_inputs, train_grads, bench_inputs, bench_grads, answer_mask, factors, precond):
    factor = factors[0]
    factor_width = factor.shape[1] // 2
    length = train_inputs.shape[2]
    masked = bench_grads[0] * answer_mask.astype(jnp.bfloat16)[:, :, None]
    train_rows = project(train_inputs[0], train_grads[0], factor)
    bench_rows = project(bench_inputs[0], masked, factor)
    tensor_count = lax.axis_size("tensor")
    train_each = train_inputs.shape[1] // tensor_count
    bench_each = bench_inputs.shape[1] // tensor_count
    row_width = train_rows.shape[1]
    blocks = jnp.concatenate(
        [
            train_rows.reshape(tensor_count, train_each * length, row_width),
            bench_rows.reshape(tensor_count, bench_each * length, row_width),
        ],
        axis=1,
    ).reshape(-1, row_width)
    share_rows = blocks.shape[0] // tensor_count
    summed = lax.psum(blocks, "tensor")
    own_rows = lax.dynamic_slice_in_dim(
        summed, lax.axis_index("tensor") * share_rows, share_rows, 0
    )
    train_feats = outer_features(own_rows[: train_each * length], train_each, length, factor_width)
    bench_feats = outer_features(own_rows[train_each * length :], bench_each, length, factor_width)
    columns = precond[0]
    pre_cols = jnp.dot(
        lax.all_gather(bench_feats, ("dp", "tensor"), axis=0, tiled=True),
        columns,
        preferred_element_type=jnp.float32,
    ).astype(jnp.bfloat16)
    layer_total = lax.axis_size("layer") * train_inputs.shape[0]
    score_scale = 1.0 / math.sqrt(factor_width * factor_width * layer_total)
    whole_pre = lax.all_gather(pre_cols, ("dp", "tensor"), axis=1, tiled=True)
    partial_value = jnp.einsum(
        "ek,jk->ej", train_feats, whole_pre, preferred_element_type=jnp.float32
    )
    scores = lax.psum_scatter(partial_value, "layer", scatter_dimension=0, tiled=True)
    return scores * score_scale


def fused_kernel(
    dims,
    ti, tg, bi, bg, mask, fac, pre,
    out,
    bench_v, train_v, fac_v, mask_v, pre_v,
    bench_part, bench_recv, train_part, train_recv,
    feats, proj, spread_v, t_send, t_all, partial_v, both_v, pair_recv, score_recv,
    load_sem, swap_send, swap_recv, feat_send, feat_recv, fwd_send,
    t_send_sem, t_recv_sem, score_send, score_recv_sem,
):
    n_dp, scale = dims
    f32, bf16 = jnp.float32, jnp.bfloat16
    z, x, layer = lax.axis_index("dp"), lax.axis_index("tensor"), lax.axis_index("layer")
    other = 1 - x
    slots = 2 * n_dp
    me = z * 2 + x
    bench_rows = bench_v.shape[2]
    train_rows = train_v.shape[2]
    length = mask.shape[1]
    width = 64
    span = 512
    columns = pre_v.shape[1]

    def load(source, target, index):
        return pltpu.make_async_copy(source, target, load_sem.at[index])

    def half(ref, position, rows):
        return ref.at[pl.ds(pl.multiple_of(position * rows, rows), rows), :]

    fac_load = load(fac, fac_v, 0)
    mask_load = load(mask, mask_v, 1)
    bench_loads = [
        load(half(ref, at, bench_rows), bench_v.at[h, i], 2 + 2 * h + i)
        for h, at in enumerate((other, x)) for i, ref in enumerate((bi, bg))
    ]
    train_loads = [
        load(half(ref, at, train_rows), train_v.at[h, i], 6 + 2 * h + i)
        for h, at in enumerate((other, x)) for i, ref in enumerate((ti, tg))
    ]
    pre_load = load(pre, pre_v, 10)
    fac_load.start()
    for one in bench_loads:
        one.start()
    mask_load.start()
    for one in train_loads:
        one.start()
    pre_load.start()

    steps = [(dz, dx) for dz in range(n_dp) for dx in range(2)]
    barrier = pltpu.get_barrier_semaphore()
    partners = [
        {"dp": lax.rem(z + dz, n_dp), "tensor": lax.rem(x + dx, 2)} for dz, dx in steps if dz or dx
    ]
    partners.append({"layer": 1 - layer})
    for partner in partners:
        pl.semaphore_signal(barrier, inc=1, device_id=partner, device_id_type=MESH)

    def build(k, carry):
        row = lax.broadcasted_iota(jnp.int32, (256, 256), 0)
        column = lax.broadcasted_iota(jnp.int32, (256, 256), 1) + k * 256
        hit = (row % 128) * width - width * width == column - column % width
        spread_v[:, pl.ds(pl.multiple_of(k * 256, 256), 256)] = jnp.where(hit, 1.0, 0.0).astype(bf16)
        return carry

    lax.fori_loop(0, spread_v.shape[1] // 256, build, 0)

    def project(ref, rows):
        both = jnp.dot(
            ref[...].reshape(2 * rows, ref.shape[2]), fac_v[...], preferred_element_type=f32
        )
        lane = lax.broadcasted_iota(jnp.int32, (rows, 128), 1)
        return jnp.where(lane < width, both[:rows], both[rows:])

    bench_swap = pltpu.make_async_remote_copy(
        bench_part.at[0], bench_recv, swap_send.at[0], swap_recv.at[0],
        device_id={"tensor": other}, device_id_type=MESH,
    )
    train_swap = pltpu.make_async_remote_copy(
        train_part.at[0], train_recv, swap_send.at[1], swap_recv.at[1],
        device_id={"tensor": other}, device_id_type=MESH,
    )

    fac_load.wait()
    bench_loads[0].wait()
    bench_loads[1].wait()
    bench_part[0] = project(bench_v.at[0], bench_rows)
    pl.semaphore_wait(barrier, slots)
    bench_swap.start()
    bench_loads[2].wait()
    bench_loads[3].wait()
    bench_part[1] = project(bench_v.at[1], bench_rows)
    train_loads[0].wait()
    train_loads[1].wait()
    train_part[0] = project(train_v.at[0], train_rows)
    train_swap.start()

    lane = lax.broadcasted_iota(jnp.int32, (8, 128), 1)

    def token_rows(own, recv, base):
        rows = []
        for t in range(length):
            window = pl.ds(base + t, 8, stride=length)
            rows.append(own[window, :] + recv[window, :])
        return rows

    def doubled(row):
        return jnp.where(lane < width, row, pltpu.roll(row, width, 1))

    def split(rows):
        whole = jnp.concatenate(rows, axis=0)
        high = whole.astype(bf16)
        low = (whole - high.astype(f32)).astype(bf16)
        return jnp.concatenate([high, low], axis=1)

    def outer(parts, seconds, start, span):
        spread = jnp.dot(
            parts, spread_v[: parts.shape[1], pl.ds(pl.multiple_of(start, span), span)], preferred_element_type=f32
        )
        values = []
        for first in range(0, len(seconds), length):
            lanes = []
            for j in range(0, span, 128):
                total = None
                for t in range(first, first + length):
                    term = spread[t * 8 : t * 8 + 8, j : j + 128] * seconds[t]
                    total = term if total is None else total + term
                lanes.append(total)
            values.append(jnp.concatenate(lanes, axis=1))
        return jnp.concatenate(values, axis=0) * (1.0 / math.sqrt(length))

    mask_load.wait()
    bench_swap.wait_recv()
    keep = mask_v[pl.ds(pl.multiple_of(x * 8, 8), 8), :].astype(f32)
    rows = token_rows(bench_part.at[1], bench_recv, 0)
    seconds = [doubled(row) for row in rows]
    masked = [jnp.where(lane < width, row, row * keep[:, t : t + 1]) for t, row in enumerate(rows)]
    proj[me] = jnp.concatenate(masked, axis=0).astype(bf16)

    def proj_copy(slot, send_sem, device_id):
        return pltpu.make_async_remote_copy(
            proj.at[slot], proj.at[slot], send_sem, feat_recv.at[slot],
            device_id=device_id, device_id_type=MESH,
        )

    sent = [proj_copy(me, feat_send.at[dz], {"dp": lax.rem(z + dz, n_dp)}) for dz in range(1, n_dp)]
    sent.append(proj_copy(me, feat_send.at[0], {"tensor": other}))
    for one in sent:
        one.start()

    train_loads[2].wait()
    train_loads[3].wait()
    train_part[1] = project(train_v.at[1], train_rows)

    def bench_slot(slot):
        tokens = proj[slot]
        bench_seconds = [doubled(tokens[t * 8 : t * 8 + 8].astype(f32)) for t in range(length)]

        def bench_block(k, carry):
            start = pl.multiple_of(k * span, span)
            feats[slot, :, pl.ds(start, span)] = outer(tokens, bench_seconds, start, span)
            return carry

        lax.fori_loop(0, feats.shape[2] // span, bench_block, 0, unroll=True)

    bench_slot(me)

    for dz in range(1, n_dp):
        one = proj_copy(lax.rem(z + n_dp - dz, n_dp) * 2 + x, fwd_send.at[dz], {"tensor": other})
        one.wait_recv()
        one.start()
        sent.append(one)

    train_swap.wait_recv()
    rows = []
    for part in range(0, t_send.shape[1], 8):
        rows += token_rows(train_part.at[1], train_recv, part * length)
    train_seconds = [doubled(row) for row in rows]
    train_split = split(rows)

    def train_block(slot, carry):
        t_send[slot] = outer(train_split, train_seconds, slot * columns, columns).astype(bf16)
        return carry

    lax.fori_loop(0, slots, train_block, 0, unroll=4)

    def t_copy(r, dz, dx):
        target = lax.rem(z + dz, n_dp) * 2 + lax.rem(x + dx, 2)
        return pltpu.make_async_remote_copy(
            t_send.at[target], t_all.at[r], t_send_sem.at[r], t_recv_sem.at[r],
            device_id={"dp": lax.rem(z + dz, n_dp), "tensor": lax.rem(x + dx, 2)}, device_id_type=MESH,
        )

    t_copies = [t_copy(r, dz, dx) for r, (dz, dx) in enumerate(steps) if r]
    for one in t_copies:
        one.start()
    t_all[0] = t_send[me]

    def own_column(dz, carry):
        bench_slot(lax.rem(z + n_dp - dz, n_dp) * 2 + x)
        return carry

    lax.fori_loop(1, n_dp, own_column, 0)

    def other_column(dz, carry):
        slot = lax.rem(z + n_dp - dz, n_dp) * 2 + other
        proj_copy(slot, feat_send.at[0], {"tensor": other}).wait_recv()
        bench_slot(slot)
        return carry

    lax.fori_loop(0, n_dp, other_column, 0)

    pre_load.wait()
    total = jnp.dot(
        feats[...].reshape(slots * 8, feats.shape[2]).astype(bf16), pre_v[...], preferred_element_type=f32
    )
    bench_pre = jnp.concatenate([total, jnp.zeros((128 - slots * 8, columns), f32)], axis=0)
    pre_high = bench_pre.astype(bf16)
    pre_low = (bench_pre - pre_high.astype(f32)).astype(bf16)

    for one in t_copies:
        one.wait_recv()
    examples = t_all.shape[1]
    held = t_all[...].reshape(slots * examples, columns)
    along = (((1,), (1,)), ((), ()))
    scores = lax.dot_general(held, pre_high, along, preferred_element_type=f32)
    scores += lax.dot_general(held, pre_low, along, preferred_element_type=f32)
    scores = scores.reshape(slots, 2, 8, 128)
    for which in range(2):
        partial_v[which] = scores[:, which]
    pair = pltpu.make_async_remote_copy(
        partial_v.at[1 - layer], pair_recv, score_send.at[0], score_recv_sem.at[0],
        device_id={"layer": 1 - layer}, device_id_type=MESH,
    )
    pair.start()
    pair.wait_recv()
    both_v[...] = partial_v[layer] + pair_recv[...]
    score_copies = []
    for r, (dz, dx) in enumerate(steps):
        if r:
            score_copies.append(
                pltpu.make_async_remote_copy(
                    both_v.at[r], score_recv.at[r], score_send.at[r], score_recv_sem.at[r],
                    device_id={"dp": lax.rem(z + n_dp - dz, n_dp), "tensor": lax.rem(x + dx, 2)},
                    device_id_type=MESH,
                )
            )
    for one in score_copies:
        one.start()
    result = both_v[0]
    for index, one in enumerate(score_copies):
        one.wait_recv()
        result = result + score_recv[index + 1]
    out[...] = result[:, : out.shape[1]] * scale

    pair.wait_send()
    bench_swap.wait_send()
    train_swap.wait_send()
    for one in sent + t_copies + score_copies:
        one.wait_send()


def fused(train_inputs, train_grads, bench_inputs, bench_grads, answer_mask, factors, precond):
    f32, bf16 = jnp.float32, jnp.bfloat16
    _, train, length, shard = train_inputs.shape
    bench = bench_inputs.shape[1]
    n_dp = lax.axis_size("dp")
    slots = 2 * n_dp
    features, columns = precond.shape[1:]
    scale = 1.0 / math.sqrt(features * lax.axis_size("layer"))
    train_rows, bench_rows = train * length // 2, bench * length // 2
    dma = pltpu.SemaphoreType.DMA
    anywhere = pl.BlockSpec(memory_space=pl.ANY)
    return pl.pallas_call(
        functools.partial(fused_kernel, (n_dp, scale)),
        out_shape=jax.ShapeDtypeStruct((8, slots * 8), f32),
        in_specs=[anywhere] * 7,
        out_specs=pl.BlockSpec(memory_space=pltpu.VMEM),
        scratch_shapes=[
            pltpu.VMEM((2, 2, bench_rows, shard), bf16),
            pltpu.VMEM((2, 2, train_rows, shard), bf16),
            pltpu.VMEM((shard, 128), bf16),
            pltpu.VMEM((bench, length), jnp.int32),
            pltpu.VMEM((features, columns), bf16),
            pltpu.VMEM((2, bench_rows, 128), f32),
            pltpu.VMEM((bench_rows, 128), f32),
            pltpu.VMEM((2, train_rows, 128), f32),
            pltpu.VMEM((train_rows, 128), f32),
            pltpu.VMEM((slots, 8, features), f32),
            pltpu.VMEM((slots, bench_rows, 128), bf16),
            pltpu.VMEM((256, features), bf16),
            pltpu.VMEM((slots, train // 2, columns), bf16),
            pltpu.VMEM((slots, train // 2, columns), bf16),
            pltpu.VMEM((2, slots, 8, 128), f32),
            pltpu.VMEM((slots, 8, 128), f32),
            pltpu.VMEM((slots, 8, 128), f32),
            pltpu.VMEM((slots, 8, 128), f32),
            dma((11,)),
            dma((2,)),
            dma((2,)),
            dma((n_dp,)),
            dma((slots,)),
            dma((n_dp,)),
            dma((slots,)),
            dma((slots,)),
            dma((slots,)),
            dma((slots,)),
        ],
        compiler_params=pltpu.CompilerParams(
            collective_id=0, has_side_effects=True, vmem_limit_bytes=56 * 1024 * 1024
        ),
    )(
        train_inputs.reshape(train * length, shard),
        train_grads.reshape(train * length, shard),
        bench_inputs.reshape(bench * length, shard),
        bench_grads.reshape(bench * length, shard),
        answer_mask,
        factors[0],
        precond[0],
    )


def fits(shapes, sizes):
    train, bench, length, shard, half_width, features, columns, layers = shapes
    n_dp, n_tensor, n_layer = sizes
    return (
        n_tensor == 2 and n_layer == 2 and layers == 1 and half_width == 64 and length == 16
        and bench == 16 and train == 32 and n_dp * 16 <= 128
        and shard % 256 == 0 and columns % 128 == 0 and features == 4096
        and features == 2 * n_dp * columns
    )


def local_any(*args):
    train_inputs, _, bench_inputs, _, _, factors, precond = args
    shapes = (
        train_inputs.shape[1], bench_inputs.shape[1], train_inputs.shape[2], train_inputs.shape[3],
        factors.shape[2] // 2, precond.shape[1], precond.shape[2], train_inputs.shape[0],
    )
    sizes = tuple(lax.axis_size(name) for name in ("dp", "tensor", "layer"))
    return fused(*args) if fits(shapes, sizes) else local(*args)


def solution(mesh):
    placed = (
        P("layer", ("groups", "dp"), None, "tensor"),
        P("layer", ("groups", "dp"), None, "tensor"),
        P("layer", ("groups", "dp"), None, "tensor"),
        P("layer", ("groups", "dp"), None, "tensor"),
        P(("groups", "dp"), None),
        P("layer", "tensor", None),
        P("layer", None, ("dp", "tensor")),
    )
    return jax.shard_map(
        local_any,
        mesh=mesh,
        in_specs=placed,
        out_specs=P(("groups", "dp", "tensor", "layer"), None),
        check_vma=False,
    )
```
